512 devices in a mesh: seg: 4 (over y_hi, core), pan: 128 (over y_lo, z, x).
Axes of the slice: x: 4, y: 8 (y_hi: 2, y_lo: 4; y = y_hi * 4 + y_lo), z: 8, core: 2. Of those that a mesh axis runs over, the one named last changes fastest.
Arguments:
- sources: bfloat16 [2, 2, 64, 1048576], P(None, None, 'seg', 'pan'), may hold values from -0.75 to 0.75
- panel_geom: float32 [6, 1048576], P(None, 'pan'), may hold values from -1 to 1, as said below
- mic_pos: float32 [3, 1024], replicated, may hold values from -12 to 12, as said below
- mic_order: int32 [1024], replicated, may hold values from 0 to 1023, each once
Outputs:
- csm: float32 [2, 1024, 1024], P(None, 'pan', 'seg')
The draws below stay inside these ranges and needn't reach their ends.
Inputs may be any that keep to these rules, and one draw needn't show every extreme that they name: `mic_order`: each of the 1024 microphones stands exactly once. `panel_geom`: panel centres lie on a cylinder of radius 1 around the first axis with first coordinate within -1 to 1; normals are the unit radial directions. `mic_pos`: microphones lie at distances 6 to 12 from the anchor (0, 0, 0).
All inputs are finite; a program needn't handle non-finite values.
Results may differ from the reference program's by a relative error of at most 0.0039.
Values may be sent and summed in bfloat16 or wider, within the bound.
No kernel may reach another device: no remote copies, remote signals or barrier semaphores. Data moves between devices by JAX's collectives and lax.ppermute only.
A program may use at most 64 MiB of HBM per device.

```python
import math
import jax
import jax.numpy as jnp
from jax import lax

M = 1024
PAN_DEV = 8192
SEGS = 64
PANELS = 1048576
N_PAN = 128


def draw_panel_geom(key, part):
    key_angle = jax.random.fold_in(key, 11)
    key_axial = jax.random.fold_in(key, 12)
    angle = jax.random.uniform(key_angle, (PANELS,), jnp.float32, -math.pi, math.pi)
    axial = jax.random.uniform(key_axial, (PANELS,), jnp.float32, -1.0, 1.0)
    cosine = jnp.cos(angle)
    sine = jnp.sin(angle)
    return jnp.stack([axial, cosine, sine, jnp.zeros_like(axial), cosine, sine]).astype(jnp.float32)


def draw_mic_pos(key, part):
    key_polar = jax.random.fold_in(key, 21)
    key_azimuth = jax.random.fold_in(key, 22)
    key_radius = jax.random.fold_in(key, 23)
    polar = jax.random.uniform(key_polar, (M,), jnp.float32, -1.0, 1.0)
    azimuth = jax.random.uniform(key_azimuth, (M,), jnp.float32, -math.pi, math.pi)
    radius = jax.random.uniform(key_radius, (M,), jnp.float32, 6.0, 12.0)
    across = jnp.sqrt(jnp.maximum(1.0 - polar * polar, 0.0))
    return jnp.stack([radius * polar, radius * across * jnp.cos(azimuth), radius * across * jnp.sin(azimuth)]).astype(jnp.float32)


def block_scale(key, extent, pieces, least, largest):
    loudness = 1.0
    for dim, blocks in pieces:
        draws = jax.random.uniform(jax.random.fold_in(jax.random.fold_in(key, 6), dim), (blocks,), jnp.float32, least / len(pieces), largest / len(pieces))
        loudness = loudness * jnp.repeat(jnp.exp(draws), extent[dim] // blocks).reshape((-1,) + (1,) * (len(extent) - 1 - dim))
    return loudness


def normal_values(rng, extent, scale, limit, cuts=(), held_as=jnp.bfloat16):
    level = block_scale(rng, extent, cuts, -0.22, 0.18) if cuts else 1.0
    values = jax.random.normal(rng, extent, jnp.float32) * scale * level
    return jnp.minimum(jnp.maximum(values, -limit), limit).astype(held_as)


def setup_inputs(seed: int = 0) -> dict:
    arg_keys = jax.random.split(jax.random.key(seed), 5)
    sources = normal_values(arg_keys[0], (2, 2, SEGS, PANELS), (50.0 / (PANELS ** 0.5)), 0.75, ((2, 4), (3, 128)))
    panel_geom = draw_panel_geom(jax.random.fold_in(arg_keys[4], 71), 0)
    mic_pos = draw_mic_pos(jax.random.fold_in(arg_keys[4], 71), 0)
    mic_order = jax.random.permutation(arg_keys[3], M).astype(jnp.int32)
    return {"sources": sources, "panel_geom": panel_geom, "mic_pos": mic_pos, "mic_order": mic_order}


mach_number = 0.3
beta_sq = 0.91
wave_number = 40.0

def kernel_block(mics, geometry):
    dx = mics[0][:, None] - geometry[0][None, :]
    dy = mics[1][:, None] - geometry[1][None, :]
    dz = mics[2][:, None] - geometry[2][None, :]
    rstar = jnp.sqrt(dx * dx + beta_sq * (dy * dy + dz * dz))
    radius = (rstar - mach_number * dx) / beta_sq
    phase = wave_number * radius
    amplitude = 1.0 / (4.0 * math.pi * rstar)
    green_re = amplitude * jnp.cos(phase)
    green_im = -amplitude * jnp.sin(phase)
    normal_part = (dx * geometry[3][None, :] + dy * geometry[4][None, :] + dz * geometry[5][None, :]) / rstar
    scale_re = normal_part / (wave_number * rstar)
    scale_im = normal_part
    dip_re = scale_re * green_re - scale_im * green_im
    dip_im = scale_re * green_im + scale_im * green_re
    return jnp.concatenate([green_re, green_im, dip_re, dip_im], axis=1).astype(jnp.bfloat16)

def build_sources(sources, blocks):
    swapped = jnp.transpose(sources, (0, 1, 3, 2))
    width = swapped.shape[2] // blocks
    swapped = swapped.reshape(2, 2, blocks, width, swapped.shape[3])
    mono_re = swapped[0, 0]
    dipole_re = swapped[0, 1]
    mono_im = swapped[1, 0]
    dipole_im = swapped[1, 1]
    real_cols = jnp.concatenate([mono_re, -mono_im, dipole_re, -dipole_im], axis=1)
    imag_cols = jnp.concatenate([mono_im, mono_re, dipole_im, dipole_re], axis=1)
    return jnp.concatenate([real_cols, imag_cols], axis=2)

def reference(sources, panel_geom, mic_pos, mic_order):
    ordered = jnp.take(mic_pos, mic_order, axis=1)
    geom_blocks = jnp.transpose(panel_geom.reshape(6, N_PAN, PAN_DEV), (1, 0, 2))
    source_blocks = build_sources(sources, N_PAN)

    def step(running, pair):
        geometry, weights = pair
        return (running + jnp.dot(kernel_block(ordered, geometry), weights, preferred_element_type=jnp.float32), None)
    init = jnp.zeros((ordered.shape[1], source_blocks.shape[2]), jnp.float32)
    spectra, unused = lax.scan(step, init, (geom_blocks, source_blocks))
    half = spectra.shape[1] // 2
    spec_re = spectra[:, :half]
    spec_im = spectra[:, half:]
    hp = lax.Precision.HIGHEST
    csm_re = jnp.dot(spec_re, spec_re.T, precision=hp) + jnp.dot(spec_im, spec_im.T, precision=hp)
    csm_im = jnp.dot(spec_im, spec_re.T, precision=hp) - jnp.dot(spec_re, spec_im.T, precision=hp)
    return jnp.stack([csm_re, csm_im]) / SEGS
```

```python
import functools
import math

import jax
import jax.numpy as jnp
from jax import lax
from jax.experimental import pallas as pl
from jax.experimental.pallas import tpu as pltpu
from jax.sharding import Mesh, PartitionSpec as P

mach_number = 0.3
beta_sq = 0.91
wave_number = 40.0
turns = wave_number / (beta_sq * 2.0 * math.pi)
half_sine = (4.44284725189209, -7.306909084320068, 3.5908987522125244, -0.7760252356529236)

f32 = jnp.float32
bf16 = jnp.bfloat16
PAN = ("yl", "z", "x")
tile = 256


def split3(value):
    high = value.astype(bf16).astype(f32)
    rest = value - high
    middle = rest.astype(bf16).astype(f32)
    return high, middle, (rest - middle).astype(bf16).astype(f32)


def zero_rows(count, width):
    return jnp.zeros((count, width), f32)


def mic_features(order_ref, mic_ref, feature_ref):
    mics = mic_ref[...]
    total = mics.shape[1]
    parts = jnp.concatenate([*split3(mics), zero_rows(7, total)], 0).astype(bf16)
    for start in range(0, total, tile):
        wanted = order_ref[:, start : start + tile]
        ids = lax.broadcasted_iota(jnp.int32, (total, tile), 0)
        chosen = jnp.where(ids == wanted, 1.0, 0.0).astype(bf16)
        picked = jnp.dot(parts, chosen, preferred_element_type=f32)
        high, middle, low = picked[0:3], picked[3:6], picked[6:9]
        full = high + middle + low
        square = (turns * turns) * (
            full[0:1] * full[0:1] + beta_sq * (full[1:2] * full[1:2] + full[2:3] * full[2:3])
        )
        shift = (-mach_number * turns) * full[0:1]
        ones = jnp.ones((3, tile), f32)
        rows = [high, high, middle, high, middle, low, ones, *split3(square), *split3(shift)]
        rows.append(zero_rows(37, tile))
        feature_ref[start : start + tile, :] = jnp.concatenate(rows, 0).T.astype(bf16)


def panel_features(geometry):
    centre, normal = geometry[0:3], geometry[3:6]
    width = geometry.shape[1]
    scale = turns * turns
    cross = jnp.concatenate(
        [centre[0:1] * (-2.0 * scale), centre[1:3] * (-2.0 * beta_sq * scale)], 0
    )
    square = scale * (
        centre[0:1] * centre[0:1]
        + beta_sq * (centre[1:2] * centre[1:2] + centre[2:3] * centre[2:3])
    )
    product = centre * normal
    offset = (-turns) * (product[0:1] + product[1:2] + product[2:3])
    shift = (mach_number * turns) * centre[0:1]
    ch, cm, cl = split3(cross)
    nh, nm, nl = split3(turns * normal)
    ones = jnp.ones((3, width), f32)

    def stack(*rows):
        used = sum(row.shape[0] for row in rows)
        return jnp.concatenate([*rows, zero_rows(64 - used, width)], 0).astype(bf16)

    distance = stack(ch, cm, ch, cl, cm, ch, *split3(square), ones)
    along = stack(nh, nm, nh, nl, nm, nh, *split3(offset))
    moved = stack(zero_rows(18, width), *split3(shift), zero_rows(3, width), ones)
    return distance, along, moved


def kernel_values(distance, along, moved):
    inverse = lax.rsqrt(distance)
    phase = distance * inverse + moved
    part = phase - jnp.round(phase)
    square = part * part
    a0, a1, a2, a3 = half_sine
    sine = part * (a0 + square * (a1 + square * (a2 + square * a3)))
    cos_all = 1.0 - sine * sine
    rest = cos_all + 1.0
    sin_all = sine * (rest * lax.rsqrt(rest))
    amplitude = inverse * (turns / (4.0 * math.pi))
    green_re = amplitude * cos_all
    green_im = amplitude * sin_all
    near = inverse * (turns / wave_number)
    normal_part = along * inverse
    dip_re = normal_part * (near * green_re + green_im)
    dip_im = normal_part * (green_re - near * green_im)
    return green_re, green_im, dip_re, dip_im


def spectra_kernel(core_ref, own_ref, other_ref, geom_ref, mic_ref, order_ref, out_ref,
                   feature_ref, total_ref, kernel_ref, weight_ref):
    panels = other_ref.shape[3]
    mics = mic_ref.shape[1]
    core = core_ref[0]
    mic_features(order_ref, mic_ref, feature_ref)
    total_ref[...] = jnp.zeros_like(total_ref)

    def step(index, carry):
        here = pl.multiple_of(core * panels + index * tile, tile)
        there = pl.multiple_of(index * tile, tile)
        distance_rows, along_rows, moved_rows = panel_features(geom_ref[:, pl.ds(here, tile)])

        def both(part, kind):
            own = own_ref[part, kind, :, pl.ds(here, tile)]
            other = other_ref[part, kind, :, pl.ds(there, tile)]
            return [jnp.where(core == 0, own, other), jnp.where(core == 0, other, own)]

        mono_re, mono_im, dip_re, dip_im = both(0, 0), both(1, 0), both(0, 1), both(1, 1)
        blocks = (
            mono_re + mono_im,
            mono_im + [-x for x in mono_re],
            dip_re + dip_im,
            [-x for x in dip_im] + dip_re,
        )
        for place, block in enumerate(blocks):
            weight_ref[:, place * tile : (place + 1) * tile] = jnp.concatenate(block, 0)
        features = feature_ref[...]
        values = kernel_values(
            jnp.dot(features, distance_rows, preferred_element_type=f32),
            jnp.dot(features, along_rows, preferred_element_type=f32),
            jnp.dot(features, moved_rows, preferred_element_type=f32),
        )
        for place, value in enumerate(values):
            kernel_ref[:, place * tile : (place + 1) * tile] = value.astype(bf16)
        total_ref[...] += lax.dot_general(
            kernel_ref[...], weight_ref[...], (((1,), (1,)), ((), ())), preferred_element_type=f32
        )
        return carry

    lax.fori_loop(0, panels // tile, step, 0)
    rows = mics // 8
    for pair in range(4):
        first = total_ref[(2 * pair) * rows : (2 * pair + 1) * rows]
        second = total_ref[(2 * pair + 1) * rows : (2 * pair + 2) * rows]
        block = jnp.concatenate([first, second], 1)
        out_ref[:rows, pair, :] = block
        out_ref[rows:, pair, :] = block


def partial_spectra(core, own, other, geometry, mic_pos, order):
    mics = mic_pos.shape[1]
    vmem = pl.BlockSpec(memory_space=pltpu.VMEM)
    return pl.pallas_call(
        spectra_kernel,
        out_shape=jax.ShapeDtypeStruct((mics // 4, 4, 128), f32),
        in_specs=[pl.BlockSpec(memory_space=pltpu.SMEM)] + [vmem] * 5,
        out_specs=vmem,
        scratch_shapes=[
            pltpu.VMEM((mics, 64), bf16),
            pltpu.VMEM((mics, 64), f32),
            pltpu.VMEM((mics, 4 * tile), bf16),
            pltpu.VMEM((64, 4 * tile), bf16),
        ],
        compiler_params=pltpu.CompilerParams(vmem_limit_bytes=40 << 20),
    )(core, own, other, geometry, mic_pos, order)


def shards(sources, panel_geom, mic_pos, mic_order):
    core = lax.axis_index("core")
    half = sources.shape[3] // 2
    away = lax.dynamic_slice_in_dim(sources, (1 - core) * half, half, 3)
    other = lax.ppermute(away, "core", [(0, 1), (1, 0)])
    order = mic_order.reshape(-1, 8).T.reshape(1, -1)
    partial = partial_spectra(
        core.astype(jnp.int32).reshape(1), sources, other, panel_geom, mic_pos, order
    )
    arrived = lax.all_to_all(partial, ("core", *PAN), 0, 0, tiled=True)
    owned = jnp.sum(arrived, axis=0)
    spread = jnp.broadcast_to(owned[None], arrived.shape)
    gathered = lax.all_to_all(spread, ("yh", *PAN), 0, 0, tiled=True)
    pan = lax.axis_index(PAN)
    quarter = lax.axis_index("yh") * 2 + core
    peers = gathered.shape[0] // 2
    gathered = gathered.reshape(2, peers, 4, 128)
    rows = lax.dynamic_slice_in_dim(gathered, pan, 1, 1).reshape(2, 8, 64)
    columns = lax.dynamic_slice_in_dim(gathered, quarter * (peers // 4), peers // 4, 1)
    columns = columns.reshape(2, 2 * peers, 64)
    turned = jnp.concatenate([rows[..., 32:], -rows[..., :32]], 2)
    left = jnp.concatenate([rows, turned], 1)
    csm = lax.dot_general(
        left, columns, (((0, 2), (0, 2)), ((), ())), precision=lax.Precision.HIGHEST
    )
    return csm.reshape(2, 8, -1) / 64


def solution(mesh):
    fine = Mesh(mesh.devices.reshape(2, 2, 4, 8, 4), ("yh", "core", *PAN))
    seg = ("yh", "core")
    placed = (P(None, None, seg, PAN), P(None, PAN), P(), P())
    return jax.shard_map(
        shards, mesh=fine, in_specs=placed, out_specs=P(None, PAN, seg), check_vma=False
    )
```

```python
import functools
import math

import jax
import jax.numpy as jnp
from jax import lax
from jax.experimental import pallas as pl
from jax.experimental.pallas import tpu as pltpu
from jax.sharding import Mesh, PartitionSpec as P

mach_number = 0.3
beta_sq = 0.91
wave_number = 40.0
turns = wave_number / (beta_sq * 2.0 * math.pi)
half_sine = (4.44284725189209, -7.306909084320068, 3.5908987522125244, -0.7760252356529236)

f32 = jnp.float32
bf16 = jnp.bfloat16
PAN = ("yl", "z", "x")
tile = 256


def split3(value):
    high = value.astype(bf16).astype(f32)
    rest = value - high
    middle = rest.astype(bf16).astype(f32)
    return high, middle, (rest - middle).astype(bf16).astype(f32)


def zero_rows(count, width):
    return jnp.zeros((count, width), f32)


def mic_features(order_ref, mic_ref, feature_ref):
    mics = mic_ref[...]
    total = mics.shape[1]
    parts = jnp.concatenate([*split3(mics), zero_rows(7, total)], 0).astype(bf16)
    for start in range(0, total, tile):
        wanted = order_ref[:, start : start + tile]
        ids = lax.broadcasted_iota(jnp.int32, (total, tile), 0)
        chosen = jnp.where(ids == wanted, 1.0, 0.0).astype(bf16)
        picked = jnp.dot(parts, chosen, preferred_element_type=f32)
        high, middle, low = picked[0:3], picked[3:6], picked[6:9]
        full = high + middle + low
        square = (turns * turns) * (
            full[0:1] * full[0:1] + beta_sq * (full[1:2] * full[1:2] + full[2:3] * full[2:3])
        )
        shift = (-mach_number * turns) * full[0:1]
        ones = jnp.ones((3, tile), f32)
        rows = [high, high, middle, high, middle, low, ones, *split3(square), *split3(shift)]
        rows.append(zero_rows(37, tile))
        feature_ref[start : start + tile, :] = jnp.concatenate(rows, 0).T.astype(bf16)


def panel_features(geometry):
    centre, normal = geometry[0:3], geometry[3:6]
    width = geometry.shape[1]
    scale = turns * turns
    cross = jnp.concatenate(
        [centre[0:1] * (-2.0 * scale), centre[1:3] * (-2.0 * beta_sq * scale)], 0
    )
    square = scale * (
        centre[0:1] * centre[0:1]
        + beta_sq * (centre[1:2] * centre[1:2] + centre[2:3] * centre[2:3])
    )
    product = centre * normal
    offset = (-turns) * (product[0:1] + product[1:2] + product[2:3])
    shift = (mach_number * turns) * centre[0:1]
    ch, cm, cl = split3(cross)
    nh, nm, nl = split3(turns * normal)
    ones = jnp.ones((3, width), f32)

    def stack(*rows):
        used = sum(row.shape[0] for row in rows)
        return jnp.concatenate([*rows, zero_rows(64 - used, width)], 0).astype(bf16)

    distance = stack(ch, cm, ch, cl, cm, ch, *split3(square), ones)
    along = stack(nh, nm, nh, nl, nm, nh, *split3(offset))
    moved = stack(zero_rows(18, width), *split3(shift), zero_rows(3, width), ones)
    return distance, along, moved


def kernel_values(distance, along, moved):
    inverse = lax.rsqrt(distance)
    phase = distance * inverse + moved
    part = phase - jnp.round(phase)
    square = part * part
    a0, a1, a2, a3 = half_sine
    sine = part * (a0 + square * (a1 + square * (a2 + square * a3)))
    cos_all = 1.0 - sine * sine
    rest = cos_all + 1.0
    sin_all = sine * (rest * lax.rsqrt(rest))
    amplitude = inverse * (turns / (4.0 * math.pi))
    green_re = amplitude * cos_all
    green_im = amplitude * sin_all
    near = inverse * (turns / wave_number)
    normal_part = along * inverse
    dip_re = normal_part * (near * green_re + green_im)
    dip_im = normal_part * (green_re - near * green_im)
    return green_re, green_im, dip_re, dip_im


def spectra_kernel(core_ref, own_ref, other_ref, geom_ref, mic_ref, order_ref, out_ref,
                   feature_ref, total_ref, kernel_ref, weight_ref):
    panels = other_ref.shape[3]
    mics = mic_ref.shape[1]
    core = core_ref[0]
    mic_features(order_ref, mic_ref, feature_ref)
    total_ref[...] = jnp.zeros_like(total_ref)

    def step(index, carry):
        here = pl.multiple_of(core * panels + index * tile, tile)
        there = pl.multiple_of(index * tile, tile)
        distance_rows, along_rows, moved_rows = panel_features(geom_ref[:, pl.ds(here, tile)])

        def both(part, kind):
            own = own_ref[part, kind, :, pl.ds(here, tile)]
            other = other_ref[part, kind, :, pl.ds(there, tile)]
            return [jnp.where(core == 0, own, other), jnp.where(core == 0, other, own)]

        mono_re, mono_im, dip_re, dip_im = both(0, 0), both(1, 0), both(0, 1), both(1, 1)
        blocks = (
            mono_re + mono_im,
            mono_im + [-x for x in mono_re],
            dip_re + dip_im,
            [-x for x in dip_im] + dip_re,
        )
        for place, block in enumerate(blocks):
            weight_ref[:, place * tile : (place + 1) * tile] = jnp.concatenate(block, 0)
        features = feature_ref[...]
        values = kernel_values(
            jnp.dot(features, distance_rows, preferred_element_type=f32),
            jnp.dot(features, along_rows, preferred_element_type=f32),
            jnp.dot(features, moved_rows, preferred_element_type=f32),
        )
        for place, value in enumerate(values):
            kernel_ref[:, place * tile : (place + 1) * tile] = value.astype(bf16)
        total_ref[...] += lax.dot_general(
            kernel_ref[...], weight_ref[...], (((1,), (1,)), ((), ())), preferred_element_type=f32
        )
        return carry

    lax.fori_loop(0, panels // tile, step, 0)
    half = mics // 2
    both_halves = jnp.concatenate([total_ref[:half], total_ref[half:]], 1)
    out_ref[...] = both_halves.reshape(out_ref.shape)


def partial_spectra(core, own, other, geometry, mic_pos, order):
    mics = mic_pos.shape[1]
    vmem = pl.BlockSpec(memory_space=pltpu.VMEM)
    return pl.pallas_call(
        spectra_kernel,
        out_shape=jax.ShapeDtypeStruct((32, mics // 64, 128), f32),
        in_specs=[pl.BlockSpec(memory_space=pltpu.SMEM)] + [vmem] * 5,
        out_specs=vmem,
        scratch_shapes=[
            pltpu.VMEM((mics, 64), bf16),
            pltpu.VMEM((mics, 64), f32),
            pltpu.VMEM((mics, 4 * tile), bf16),
            pltpu.VMEM((64, 4 * tile), bf16),
        ],
        compiler_params=pltpu.CompilerParams(vmem_limit_bytes=40 << 20),
    )(core, own, other, geometry, mic_pos, order)


def shards(sources, panel_geom, mic_pos, mic_order):
    core = lax.axis_index("core")
    half = sources.shape[3] // 2
    away = lax.dynamic_slice_in_dim(sources, (1 - core) * half, half, 3)
    other = lax.ppermute(away, "core", [(0, 1), (1, 0)])
    order = mic_order.reshape(2, 2, 32, 8).transpose(0, 2, 1, 3).reshape(1, -1)
    partial = partial_spectra(
        core.astype(jnp.int32).reshape(1), sources, other, panel_geom, mic_pos, order
    )
    kept = jnp.sum(lax.all_to_all(partial, ("z", "x"), 0, 0, tiled=True), axis=0)
    quarters = kept.reshape(2, 8, 2, 64).transpose(2, 0, 1, 3).reshape(4, 8, 64)
    for_columns = jnp.repeat(quarters, 4, axis=0)
    for_rows = jnp.tile(quarters, (4, 1, 1))
    terms = jnp.concatenate([for_columns, for_rows], 2)
    terms = lax.all_to_all(terms, ("yh", "core", "yl"), 0, 0, tiled=True)
    joined = jnp.sum(terms.reshape(2, 8, 8, 128), axis=1)
    rows = joined[:, :, 64:]
    own_columns = joined[:, :, :64].transpose(1, 0, 2).reshape(8, 128)
    spread = jnp.broadcast_to(own_columns[None], (32, 8, 128))
    columns = lax.all_to_all(spread, ("z", "x"), 0, 0, tiled=True).reshape(256, 128)
    turned = jnp.concatenate([rows[..., 32:], -rows[..., :32]], 2)
    left = jnp.concatenate([rows, turned], 1).transpose(1, 0, 2).reshape(16, 128)
    csm = lax.dot_general(
        left, columns, (((1,), (1,)), ((), ())), precision=lax.Precision.HIGHEST
    )
    return csm.reshape(2, 8, -1) / 64


def solution(mesh):
    fine = Mesh(mesh.devices.reshape(2, 2, 4, 8, 4), ("yh", "core", *PAN))
    seg = ("yh", "core")
    placed = (P(None, None, seg, PAN), P(None, PAN), P(), P())
    return jax.shard_map(
        shards, mesh=fine, in_specs=placed, out_specs=P(None, PAN, seg), check_vma=False
    )
```

```python
import functools
import math

import jax
import jax.numpy as jnp
from jax import lax
from jax.experimental import pallas as pl
from jax.experimental.pallas import tpu as pltpu
from jax.sharding import Mesh, PartitionSpec as P

mach_number = 0.3
beta_sq = 0.91
wave_number = 40.0
turns = wave_number / (beta_sq * 2.0 * math.pi)
half_sine = (4.44284725189209, -7.306909084320068, 3.5908987522125244, -0.7760252356529236)
strength = turns / (4.0 * math.pi)
scaled_sine = tuple(math.sqrt(strength) * value for value in half_sine)

f32 = jnp.float32
bf16 = jnp.bfloat16
PAN = ("yl", "z", "x")
tile = 256
chunk = 512
unroll = 4


def split3(value):
    high = value.astype(bf16).astype(f32)
    rest = value - high
    middle = rest.astype(bf16).astype(f32)
    return high, middle, (rest - middle).astype(bf16).astype(f32)


def zero_rows(count, width):
    return jnp.zeros((count, width), f32)


def mic_features(order_ref, mic_ref, feature_ref):
    mics = mic_ref[...]
    total = mics.shape[1]
    parts = jnp.concatenate([*split3(mics), zero_rows(7, total)], 0).astype(bf16)
    for start in range(0, total, tile):
        wanted = order_ref[:, start : start + tile]
        ids = lax.broadcasted_iota(jnp.int32, (total, tile), 0)
        chosen = jnp.where(ids == wanted, 1.0, 0.0).astype(bf16)
        picked = jnp.dot(parts, chosen, preferred_element_type=f32)
        high, middle, low = picked[0:3], picked[3:6], picked[6:9]
        full = high + middle + low
        square = (turns * turns) * (
            full[0:1] * full[0:1] + beta_sq * (full[1:2] * full[1:2] + full[2:3] * full[2:3])
        )
        shift = (-mach_number * turns) * full[0:1]
        ones = jnp.ones((3, tile), f32)
        rows = [high, high, middle, high, middle, low, ones, *split3(square), *split3(shift)]
        rows.append(zero_rows(37, tile))
        feature_ref[start : start + tile, :] = jnp.concatenate(rows, 0).T.astype(bf16)


def panel_features(geometry):
    centre, normal = geometry[0:3], geometry[3:6]
    width = geometry.shape[1]
    scale = turns * turns
    cross = jnp.concatenate(
        [centre[0:1] * (-2.0 * scale), centre[1:3] * (-2.0 * beta_sq * scale)], 0
    )
    square = scale * (
        centre[0:1] * centre[0:1]
        + beta_sq * (centre[1:2] * centre[1:2] + centre[2:3] * centre[2:3])
    )
    product = centre * normal
    offset = (-turns) * (product[0:1] + product[1:2] + product[2:3])
    shift = (mach_number * turns) * centre[0:1]
    ch, cm, cl = split3(cross)
    nh, nm, nl = split3(turns * normal)
    ones = jnp.ones((3, width), f32)

    def stack(*rows):
        used = sum(row.shape[0] for row in rows)
        return jnp.concatenate([*rows, zero_rows(64 - used, width)], 0).astype(bf16)

    distance = stack(ch, cm, ch, cl, cm, ch, *split3(square), ones)
    along = stack(nh, nm, nh, nl, nm, nh, *split3(offset))
    moved = stack(zero_rows(18, width), *split3(shift), zero_rows(3, width), ones)
    return distance, along, moved


def kernel_values(distance, along, moved):
    inverse = lax.rsqrt(distance)
    phase = distance * inverse + moved
    part = phase - jnp.round(phase)
    square = part * part
    a0, a1, a2, a3 = scaled_sine
    sine = part * (a0 + square * (a1 + square * (a2 + square * a3)))
    cos_all = strength - sine * sine
    rest = cos_all + strength
    sin_all = sine * (rest * lax.rsqrt(rest))
    green_re = inverse * cos_all
    green_im = inverse * sin_all
    near = inverse * (turns / wave_number)
    normal_part = along * inverse
    dip_re = normal_part * (near * green_re + green_im)
    dip_im = normal_part * (green_re - near * green_im)
    return green_re, green_im, dip_re, dip_im


def spectra_kernel(core_ref, own_ref, other_ref, geom_ref, mic_ref, order_ref, out_ref,
                   feature_ref, total_ref, *buffers):
    panels = other_ref.shape[3]
    mics = mic_ref.shape[1]
    core = core_ref[0]
    mic_features(order_ref, mic_ref, feature_ref)
    total_ref[...] = jnp.zeros_like(total_ref)

    def block_of_panels(index, kernel_ref, weight_ref):
        here = pl.multiple_of(core * panels + index * tile, tile)
        there = pl.multiple_of(index * tile, tile)
        distance_rows, along_rows, moved_rows = panel_features(geom_ref[:, pl.ds(here, tile)])

        def both(part, kind):
            own = own_ref[part, kind, :, pl.ds(here, tile)]
            other = other_ref[part, kind, :, pl.ds(there, tile)]
            return [jnp.where(core == 0, own, other), jnp.where(core == 0, other, own)]

        mono_re, mono_im, dip_re, dip_im = both(0, 0), both(1, 0), both(0, 1), both(1, 1)
        blocks = (
            mono_re + mono_im,
            mono_im + [-x for x in mono_re],
            dip_re + dip_im,
            [-x for x in dip_im] + dip_re,
        )
        for place, block in enumerate(blocks):
            weight_ref[:, place * tile : (place + 1) * tile] = jnp.concatenate(block, 0)
        for start in range(0, mics, chunk):
            rows = slice(start, start + chunk)
            features = feature_ref[rows]
            distance = jnp.dot(features, distance_rows, preferred_element_type=f32)
            moved = jnp.dot(features, moved_rows, preferred_element_type=f32)
            along = jnp.dot(features, along_rows, preferred_element_type=f32)
            for place, value in enumerate(kernel_values(distance, along, moved)):
                kernel_ref[rows, place * tile : (place + 1) * tile] = value.astype(bf16)
        total_ref[...] += lax.dot_general(
            kernel_ref[...], weight_ref[...], (((1,), (1,)), ((), ())), preferred_element_type=f32
        )

    def step(index, carry):
        for part in range(unroll):
            kernel_ref, weight_ref = buffers[2 * (part % 2) : 2 * (part % 2) + 2]
            block_of_panels(unroll * index + part, kernel_ref, weight_ref)
        return carry

    lax.fori_loop(0, panels // (unroll * tile), step, 0)
    half = mics // 2
    both_halves = jnp.concatenate([total_ref[:half], total_ref[half:]], 1)
    out_ref[...] = both_halves.reshape(out_ref.shape)


def partial_spectra(core, own, other, geometry, mic_pos, order):
    mics = mic_pos.shape[1]
    vmem = pl.BlockSpec(memory_space=pltpu.VMEM)
    return pl.pallas_call(
        spectra_kernel,
        out_shape=jax.ShapeDtypeStruct((32, mics // 64, 128), f32),
        in_specs=[pl.BlockSpec(memory_space=pltpu.SMEM)] + [vmem] * 5,
        out_specs=vmem,
        scratch_shapes=[
            pltpu.VMEM((mics, 64), bf16),
            pltpu.VMEM((mics, 64), f32),
        ]
        + [pltpu.VMEM((mics, 4 * tile), bf16), pltpu.VMEM((64, 4 * tile), bf16)] * 2,
        compiler_params=pltpu.CompilerParams(vmem_limit_bytes=40 << 20),
    )(core, own, other, geometry, mic_pos, order)


def shards(sources, panel_geom, mic_pos, mic_order):
    core = lax.axis_index("core")
    half = sources.shape[3] // 2
    away = lax.dynamic_slice_in_dim(sources, (1 - core) * half, half, 3)
    other = lax.ppermute(away, "core", [(0, 1), (1, 0)])
    order = mic_order.reshape(2, 2, 32, 8).transpose(0, 2, 1, 3).reshape(1, -1)
    partial = partial_spectra(
        core.astype(jnp.int32).reshape(1), sources, other, panel_geom, mic_pos, order
    )
    kept = jnp.sum(lax.all_to_all(partial, ("z", "x"), 0, 0, tiled=True), axis=0)
    quarters = kept.reshape(2, 8, 2, 64).transpose(2, 0, 1, 3).reshape(4, 8, 64)
    for_columns = jnp.repeat(quarters, 4, axis=0)
    for_rows = jnp.tile(quarters, (4, 1, 1))
    terms = jnp.concatenate([for_columns, for_rows], 2)
    terms = lax.all_to_all(terms, ("yh", "core", "yl"), 0, 0, tiled=True)
    joined = jnp.sum(terms.reshape(2, 8, 8, 128), axis=1)
    rows = joined[:, :, 64:]
    own_columns = joined[:, :, :64].transpose(1, 0, 2).reshape(8, 128)
    spread = jnp.broadcast_to(own_columns[None], (32, 8, 128))
    columns = lax.all_to_all(spread, ("z", "x"), 0, 0, tiled=True).reshape(256, 128)
    turned = jnp.concatenate([rows[..., 32:], -rows[..., :32]], 2)
    left = jnp.concatenate([rows, turned], 1).transpose(1, 0, 2).reshape(16, 128)
    csm = lax.dot_general(
        left, columns, (((1,), (1,)), ((), ())), precision=lax.Precision.HIGHEST
    )
    return csm.reshape(2, 8, -1) / 64


def solution(mesh):
    fine = Mesh(mesh.devices.reshape(2, 2, 4, 8, 4), ("yh", "core", *PAN))
    seg = ("yh", "core")
    placed = (P(None, None, seg, PAN), P(None, PAN), P(), P())
    return jax.shard_map(
        shards, mesh=fine, in_specs=placed, out_specs=P(None, PAN, seg), check_vma=False
    )
```

```python
import functools
import math

import jax
import jax.numpy as jnp
from jax import lax
from jax.experimental import pallas as pl
from jax.experimental.pallas import tpu as pltpu
from jax.sharding import Mesh, PartitionSpec as P

mach_number = 0.3
beta_sq = 0.91
wave_number = 40.0
turns = wave_number / (beta_sq * 2.0 * math.pi)
half_sine = (4.44284725189209, -7.306909084320068, 3.5908987522125244, -0.7760252356529236)
strength = turns / (4.0 * math.pi)
scaled_sine = tuple(math.sqrt(strength) * value for value in half_sine)

f32 = jnp.float32
bf16 = jnp.bfloat16
PAN = ("yl", "z", "x")
tile = 256
chunk = 512
unroll = 4


def split3(value):
    high = value.astype(bf16).astype(f32)
    rest = value - high
    middle = rest.astype(bf16).astype(f32)
    return high, middle, (rest - middle).astype(bf16).astype(f32)


def zero_rows(count, width):
    return jnp.zeros((count, width), f32)


def mic_features(order_ref, mic_ref, feature_ref):
    mics = mic_ref[...]
    total = mics.shape[1]
    parts = jnp.concatenate([*split3(mics), zero_rows(7, total)], 0).astype(bf16)
    for start in range(0, total, tile):
        wanted = order_ref[:, start : start + tile]
        ids = lax.broadcasted_iota(jnp.int32, (total, tile), 0)
        chosen = jnp.where(ids == wanted, 1.0, 0.0).astype(bf16)
        picked = jnp.dot(parts, chosen, preferred_element_type=f32)
        high, middle, low = picked[0:3], picked[3:6], picked[6:9]
        full = high + middle + low
        square = (turns * turns) * (
            full[0:1] * full[0:1] + beta_sq * (full[1:2] * full[1:2] + full[2:3] * full[2:3])
        )
        shift = (-mach_number * turns) * full[0:1]
        ones = jnp.ones((3, tile), f32)
        rows = [high, high, middle, high, middle, low, ones, *split3(square), *split3(shift)]
        rows.append(zero_rows(37, tile))
        feature_ref[start : start + tile, :] = jnp.concatenate(rows, 0).T.astype(bf16)


def panel_features(geometry):
    centre, normal = geometry[0:3], geometry[3:6]
    width = geometry.shape[1]
    scale = turns * turns
    cross = jnp.concatenate(
        [centre[0:1] * (-2.0 * scale), centre[1:3] * (-2.0 * beta_sq * scale)], 0
    )
    square = scale * (
        centre[0:1] * centre[0:1]
        + beta_sq * (centre[1:2] * centre[1:2] + centre[2:3] * centre[2:3])
    )
    product = centre * normal
    offset = (-turns) * (product[0:1] + product[1:2] + product[2:3])
    shift = (mach_number * turns) * centre[0:1]
    ch, cm, cl = split3(cross)
    nh, nm, nl = split3(turns * normal)
    ones = jnp.ones((3, width), f32)

    def stack(*rows):
        used = sum(row.shape[0] for row in rows)
        return jnp.concatenate([*rows, zero_rows(64 - used, width)], 0).astype(bf16)

    distance = stack(ch, cm, ch, cl, cm, ch, *split3(square), ones)
    along = stack(nh, nm, nh, nl, nm, nh, *split3(offset))
    moved = stack(zero_rows(18, width), *split3(shift), zero_rows(3, width), ones)
    return distance, along, moved


def kernel_values(distance, along, moved):
    inverse = lax.rsqrt(distance)
    phase = distance * inverse + moved
    part = phase - jnp.round(phase)
    square = part * part
    a0, a1, a2, a3 = scaled_sine
    sine = part * (a0 + square * (a1 + square * (a2 + square * a3)))
    cos_all = strength - sine * sine
    rest = cos_all + strength
    sin_all = sine * (rest * lax.rsqrt(rest))
    green_re = inverse * cos_all
    green_im = inverse * sin_all
    near = inverse * (turns / wave_number)
    normal_part = along * inverse
    dip_re = normal_part * (near * green_re + green_im)
    dip_im = normal_part * (green_re - near * green_im)
    return green_re, green_im, dip_re, dip_im


def prepare_kernel(core_ref, geom_ref, mic_ref, order_ref, feature_ref, *panel_refs):
    mic_features(order_ref, mic_ref, feature_ref)
    panels = panel_refs[0].shape[1]
    for start in range(0, panels, chunk):
        here = pl.multiple_of(core_ref[0] * panels + start, chunk)
        for ref, rows in zip(panel_refs, panel_features(geom_ref[:, pl.ds(here, chunk)])):
            ref[:, start : start + chunk] = rows


def spectra_kernel(core_ref, own_ref, other_ref, feature_ref, distance_ref, along_ref, moved_ref,
                   out_ref, total_ref, *buffers):
    panels = distance_ref.shape[1]
    mics = feature_ref.shape[0]
    core = core_ref[0]
    total_ref[...] = jnp.zeros_like(total_ref)

    def block_of_panels(index, kernel_ref, weight_ref):
        here = pl.multiple_of(core * panels + index * tile, tile)
        columns = pl.ds(pl.multiple_of(index * tile, tile), tile)
        distance_rows, along_rows, moved_rows = (
            ref[:, columns] for ref in (distance_ref, along_ref, moved_ref)
        )

        def both(part, kind):
            own = own_ref[part, kind, :, pl.ds(here, tile)]
            other = other_ref[part, kind, :, pl.ds(here, tile)]
            return [jnp.where(core == 0, own, other), jnp.where(core == 0, other, own)]

        mono_re, mono_im, dip_re, dip_im = both(0, 0), both(1, 0), both(0, 1), both(1, 1)
        blocks = (
            mono_re + mono_im,
            mono_im + [-x for x in mono_re],
            dip_re + dip_im,
            [-x for x in dip_im] + dip_re,
        )
        for place, block in enumerate(blocks):
            weight_ref[:, place * tile : (place + 1) * tile] = jnp.concatenate(block, 0)
        for start in range(0, mics, chunk):
            rows = slice(start, start + chunk)
            features = feature_ref[rows]
            distance = jnp.dot(features, distance_rows, preferred_element_type=f32)
            moved = jnp.dot(features, moved_rows, preferred_element_type=f32)
            along = jnp.dot(features, along_rows, preferred_element_type=f32)
            for place, value in enumerate(kernel_values(distance, along, moved)):
                kernel_ref[rows, place * tile : (place + 1) * tile] = value.astype(bf16)
        total_ref[...] += lax.dot_general(
            kernel_ref[...], weight_ref[...], (((1,), (1,)), ((), ())), preferred_element_type=f32
        )

    def step(index, carry):
        for part in range(unroll):
            kernel_ref, weight_ref = buffers[2 * (part % 2) : 2 * (part % 2) + 2]
            block_of_panels(unroll * index + part, kernel_ref, weight_ref)
        return carry

    lax.fori_loop(0, panels // (unroll * tile), step, 0)
    half = mics // 2
    both_halves = jnp.concatenate([total_ref[:half], total_ref[half:]], 1)
    out_ref[...] = both_halves.reshape(out_ref.shape)


vmem = pl.BlockSpec(memory_space=pltpu.VMEM)
smem = pl.BlockSpec(memory_space=pltpu.SMEM)


def prepared(core, geometry, mic_pos, order):
    mics = mic_pos.shape[1]
    panels = geometry.shape[1] // 2
    rows = jax.ShapeDtypeStruct((64, panels), bf16)
    return pl.pallas_call(
        prepare_kernel,
        out_shape=[jax.ShapeDtypeStruct((mics, 64), bf16), rows, rows, rows],
        in_specs=[smem] + [vmem] * 3,
        out_specs=[vmem] * 4,
        compiler_params=pltpu.CompilerParams(vmem_limit_bytes=16 << 20),
        cost_estimate=pl.CostEstimate(
            flops=2 * 10**9, bytes_accessed=3000000, transcendentals=0
        ),
    )(core, geometry, mic_pos, order)


def partial_spectra(core, own, other, features):
    mics = features[0].shape[0]
    return pl.pallas_call(
        spectra_kernel,
        out_shape=jax.ShapeDtypeStruct((32, mics // 64, 128), f32),
        in_specs=[smem] + [vmem] * 6,
        out_specs=vmem,
        scratch_shapes=[pltpu.VMEM((mics, 64), f32)]
        + [pltpu.VMEM((mics, 4 * tile), bf16), pltpu.VMEM((64, 4 * tile), bf16)] * 2,
        compiler_params=pltpu.CompilerParams(vmem_limit_bytes=32 << 20),
    )(core, own, other, *features)


def shards(sources, panel_geom, mic_pos, mic_order):
    core = lax.axis_index("core")
    other = lax.ppermute(sources, "core", [(0, 1), (1, 0)])
    order = mic_order.reshape(2, 2, 32, 8).transpose(0, 2, 1, 3).reshape(1, -1)
    which = core.astype(jnp.int32).reshape(1)
    features = prepared(which, panel_geom, mic_pos, order)
    partial = partial_spectra(which, sources, other, features)
    kept = jnp.sum(lax.all_to_all(partial, ("z", "x"), 0, 0, tiled=True), axis=0)
    quarters = kept.reshape(2, 8, 2, 64).transpose(2, 0, 1, 3).reshape(4, 8, 64)
    for_columns = jnp.repeat(quarters, 4, axis=0)
    for_rows = jnp.tile(quarters, (4, 1, 1))
    terms = jnp.concatenate([for_columns, for_rows], 2)
    terms = lax.all_to_all(terms, ("yh", "core", "yl"), 0, 0, tiled=True)
    joined = jnp.sum(terms.reshape(2, 8, 8, 128), axis=1)
    rows = joined[:, :, 64:]
    own_columns = joined[:, :, :64].transpose(1, 0, 2).reshape(8, 128)
    spread = jnp.broadcast_to(own_columns[None], (32, 8, 128))
    columns = lax.all_to_all(spread, ("z", "x"), 0, 0, tiled=True).reshape(256, 128)
    turned = jnp.concatenate([rows[..., 32:], -rows[..., :32]], 2)
    left = jnp.concatenate([rows, turned], 1).transpose(1, 0, 2).reshape(16, 128)
    csm = lax.dot_general(
        left, columns, (((1,), (1,)), ((), ())), precision=lax.Precision.HIGHEST
    )
    return csm.reshape(2, 8, -1) / 64


def solution(mesh):
    fine = Mesh(mesh.devices.reshape(2, 2, 4, 8, 4), ("yh", "core", *PAN))
    seg = ("yh", "core")
    placed = (P(None, None, seg, PAN), P(None, PAN), P(), P())
    return jax.shard_map(
        shards, mesh=fine, in_specs=placed, out_specs=P(None, PAN, seg), check_vma=False
    )
```

```python
import functools
import math

import jax
import jax.numpy as jnp
from jax import lax
from jax.experimental import pallas as pl
from jax.experimental.pallas import tpu as pltpu
from jax.sharding import Mesh, PartitionSpec as P

mach_number = 0.3
beta_sq = 0.91
wave_number = 40.0
turns = wave_number / (beta_sq * 2.0 * math.pi)
half_sine = (4.44284725189209, -7.306909084320068, 3.5908987522125244, -0.7760252356529236)
strength = turns / (4.0 * math.pi)
scaled_sine = tuple(math.sqrt(strength) * value for value in half_sine)

f32 = jnp.float32
bf16 = jnp.bfloat16
PAN = ("yl", "z", "x")
tile = 256
chunk = 512
unroll = 4


def split3(value):
    high = value.astype(bf16).astype(f32)
    rest = value - high
    middle = rest.astype(bf16).astype(f32)
    return high, middle, (rest - middle).astype(bf16).astype(f32)


def zero_rows(count, width):
    return jnp.zeros((count, width), f32)


def mic_features(order_ref, mic_ref, feature_ref):
    mics = mic_ref[...]
    total = mics.shape[1]
    parts = jnp.concatenate([*split3(mics), zero_rows(7, total)], 0).astype(bf16)
    for start in range(0, total, tile):
        wanted = order_ref[:, start : start + tile]
        ids = lax.broadcasted_iota(jnp.int32, (total, tile), 0)
        chosen = jnp.where(ids == wanted, 1.0, 0.0).astype(bf16)
        picked = jnp.dot(parts, chosen, preferred_element_type=f32)
        high, middle, low = picked[0:3], picked[3:6], picked[6:9]
        full = high + middle + low
        square = (turns * turns) * (
            full[0:1] * full[0:1] + beta_sq * (full[1:2] * full[1:2] + full[2:3] * full[2:3])
        )
        shift = (-mach_number * turns) * full[0:1]
        ones = jnp.ones((3, tile), f32)
        rows = [high, high, middle, high, middle, low, ones, *split3(square), *split3(shift)]
        rows.append(zero_rows(37, tile))
        feature_ref[start : start + tile, :] = jnp.concatenate(rows, 0).T.astype(bf16)


def panel_features(geometry):
    centre, normal = geometry[0:3], geometry[3:6]
    width = geometry.shape[1]
    scale = turns * turns
    cross = jnp.concatenate(
        [centre[0:1] * (-2.0 * scale), centre[1:3] * (-2.0 * beta_sq * scale)], 0
    )
    square = scale * (
        centre[0:1] * centre[0:1]
        + beta_sq * (centre[1:2] * centre[1:2] + centre[2:3] * centre[2:3])
    )
    product = centre * normal
    offset = (-turns) * (product[0:1] + product[1:2] + product[2:3])
    shift = (mach_number * turns) * centre[0:1]
    ch, cm, cl = split3(cross)
    nh, nm, nl = split3(turns * normal)
    ones = jnp.ones((3, width), f32)

    def stack(*rows):
        used = sum(row.shape[0] for row in rows)
        return jnp.concatenate([*rows, zero_rows(64 - used, width)], 0).astype(bf16)

    distance = stack(ch, cm, ch, cl, cm, ch, *split3(square), ones)
    along = stack(nh, nm, nh, nl, nm, nh, *split3(offset))
    moved = stack(zero_rows(18, width), *split3(shift), zero_rows(3, width), ones)
    return distance, along, moved


def kernel_values(distance, along, moved):
    inverse = lax.rsqrt(distance)
    phase = distance * inverse + moved
    part = phase - jnp.round(phase)
    square = part * part
    a0, a1, a2, a3 = scaled_sine
    sine = part * (a0 + square * (a1 + square * (a2 + square * a3)))
    cos_all = strength - sine * sine
    rest = cos_all + strength
    sin_all = sine * (rest * lax.rsqrt(rest))
    green_re = inverse * cos_all
    green_im = inverse * sin_all
    near = inverse * (turns / wave_number)
    normal_part = along * inverse
    part_re = normal_part * green_re
    part_im = normal_part * green_im
    dip_re = near * part_re + part_im
    dip_im = part_re - near * part_im
    return green_re, green_im, dip_re, dip_im


def spectra_kernel(core_ref, own_ref, other_ref, geom_ref, feature_ref, out_ref, total_ref,
                   *buffers):
    panels = own_ref.shape[3] // 2
    mics = feature_ref.shape[0]
    core = core_ref[0]
    total_ref[...] = jnp.zeros_like(total_ref)

    def block_of_panels(index, kernel_ref, weight_ref):
        here = pl.multiple_of(core * panels + index * tile, tile)
        distance_rows, along_rows, moved_rows = panel_features(geom_ref[:, pl.ds(here, tile)])

        def both(part, kind):
            own = own_ref[part, kind, :, pl.ds(here, tile)]
            other = other_ref[part, kind, :, pl.ds(here, tile)]
            return [jnp.where(core == 0, own, other), jnp.where(core == 0, other, own)]

        mono_re, mono_im, dip_re, dip_im = both(0, 0), both(1, 0), both(0, 1), both(1, 1)
        blocks = (
            mono_re + mono_im,
            mono_im + [-x for x in mono_re],
            dip_re + dip_im,
            [-x for x in dip_im] + dip_re,
        )
        for place, block in enumerate(blocks):
            weight_ref[:, place * tile : (place + 1) * tile] = jnp.concatenate(block, 0)
        for start in range(0, mics, chunk):
            rows = slice(start, start + chunk)
            features = feature_ref[rows]
            distance = jnp.dot(features, distance_rows, preferred_element_type=f32)
            moved = jnp.dot(features, moved_rows, preferred_element_type=f32)
            along = jnp.dot(features, along_rows, preferred_element_type=f32)
            for place, value in enumerate(kernel_values(distance, along, moved)):
                kernel_ref[rows, place * tile : (place + 1) * tile] = value.astype(bf16)
        total_ref[...] += lax.dot_general(
            kernel_ref[...], weight_ref[...], (((1,), (1,)), ((), ())), preferred_element_type=f32
        )

    def step(index, carry):
        for part in range(unroll):
            kernel_ref, weight_ref = buffers[2 * (part % 2) : 2 * (part % 2) + 2]
            block_of_panels(unroll * index + part, kernel_ref, weight_ref)
        return carry

    lax.fori_loop(0, panels // (unroll * tile), step, 0)
    half = mics // 2
    both_halves = jnp.concatenate([total_ref[:half], total_ref[half:]], 1)
    out_ref[...] = both_halves.reshape(out_ref.shape)


vmem = pl.BlockSpec(memory_space=pltpu.VMEM)
smem = pl.BlockSpec(memory_space=pltpu.SMEM)


def prepared(mic_pos, order):
    mics = mic_pos.shape[1]
    return pl.pallas_call(
        mic_features,
        out_shape=jax.ShapeDtypeStruct((mics, 64), bf16),
        in_specs=[vmem] * 2,
        out_specs=vmem,
        compiler_params=pltpu.CompilerParams(vmem_limit_bytes=16 << 20),
        cost_estimate=pl.CostEstimate(
            flops=2 * 10**9, bytes_accessed=300000, transcendentals=0
        ),
    )(order, mic_pos)


def partial_spectra(core, own, other, geometry, features):
    mics = features.shape[0]
    return pl.pallas_call(
        spectra_kernel,
        out_shape=jax.ShapeDtypeStruct((32, mics // 64, 128), f32),
        in_specs=[smem] + [vmem] * 4,
        out_specs=vmem,
        scratch_shapes=[pltpu.VMEM((mics, 64), f32)]
        + [pltpu.VMEM((mics, 4 * tile), bf16), pltpu.VMEM((64, 4 * tile), bf16)] * 2,
        compiler_params=pltpu.CompilerParams(vmem_limit_bytes=32 << 20),
    )(core, own, other, geometry, features)


def shards(sources, panel_geom, mic_pos, mic_order):
    core = lax.axis_index("core")
    other = lax.ppermute(sources, "core", [(0, 1), (1, 0)])
    order = mic_order.reshape(2, 2, 32, 8).transpose(0, 2, 1, 3).reshape(1, -1)
    which = core.astype(jnp.int32).reshape(1)
    features = prepared(mic_pos, order)
    partial = partial_spectra(which, sources, other, panel_geom, features)
    kept = jnp.sum(lax.all_to_all(partial, ("z", "x"), 0, 0, tiled=True), axis=0)
    quarters = kept.reshape(2, 8, 2, 64).transpose(2, 0, 1, 3).reshape(4, 8, 64)
    for_columns = jnp.repeat(quarters, 4, axis=0)
    for_rows = jnp.tile(quarters, (4, 1, 1))
    terms = jnp.concatenate([for_columns, for_rows], 2)
    terms = lax.all_to_all(terms, ("yh", "core", "yl"), 0, 0, tiled=True)
    joined = jnp.sum(terms.reshape(2, 8, 8, 128), axis=1)
    rows = joined[:, :, 64:]
    own_columns = joined[:, :, :64].transpose(1, 0, 2).reshape(8, 128)
    spread = jnp.broadcast_to(own_columns[None], (32, 8, 128))
    columns = lax.all_to_all(spread, ("z", "x"), 0, 0, tiled=True).reshape(256, 128)
    turned = jnp.concatenate([rows[..., 32:], -rows[..., :32]], 2)
    left = jnp.concatenate([rows, turned], 1).transpose(1, 0, 2).reshape(16, 128)
    csm = lax.dot_general(
        left, columns, (((1,), (1,)), ((), ())), precision=lax.Precision.HIGHEST
    )
    return csm.reshape(2, 8, -1) / 64


def solution(mesh):
    fine = Mesh(mesh.devices.reshape(2, 2, 4, 8, 4), ("yh", "core", *PAN))
    seg = ("yh", "core")
    placed = (P(None, None, seg, PAN), P(None, PAN), P(), P())
    return jax.shard_map(
        shards, mesh=fine, in_specs=placed, out_specs=P(None, PAN, seg), check_vma=False
    )
```

```python
import functools
import math

import jax
import jax.numpy as jnp
from jax import lax
from jax.experimental import pallas as pl
from jax.experimental.pallas import tpu as pltpu
from jax.sharding import Mesh, PartitionSpec as P

mach_number = 0.3
beta_sq = 0.91
wave_number = 40.0
turns = wave_number / (beta_sq * 2.0 * math.pi)
half_sine = (4.44284725189209, -7.306909084320068, 3.5908987522125244, -0.7760252356529236)
strength = turns / (4.0 * math.pi)
scaled_sine = tuple(math.sqrt(strength) * value for value in half_sine)

f32 = jnp.float32
bf16 = jnp.bfloat16
PAN = ("yl", "z", "x")
tile = 256
chunk = 512
unroll = 5


def split3(value):
    high = value.astype(bf16).astype(f32)
    rest = value - high
    middle = rest.astype(bf16).astype(f32)
    return high, middle, (rest - middle).astype(bf16).astype(f32)


def zero_rows(count, width):
    return jnp.zeros((count, width), f32)


def mic_features(order_ref, mic_ref, feature_ref):
    mics = mic_ref[...]
    total = mics.shape[1]
    parts = jnp.concatenate([*split3(mics), zero_rows(7, total)], 0).astype(bf16)
    for start in range(0, total, tile):
        wanted = order_ref[:, start : start + tile]
        ids = lax.broadcasted_iota(jnp.int32, (total, tile), 0)
        chosen = jnp.where(ids == wanted, 1.0, 0.0).astype(bf16)
        picked = jnp.dot(parts, chosen, preferred_element_type=f32)
        high, middle, low = picked[0:3], picked[3:6], picked[6:9]
        full = high + middle + low
        square = (turns * turns) * (
            full[0:1] * full[0:1] + beta_sq * (full[1:2] * full[1:2] + full[2:3] * full[2:3])
        )
        shift = (-mach_number * turns) * full[0:1]
        ones = jnp.ones((3, tile), f32)
        rows = [high, high, middle, high, middle, low, ones, *split3(square), *split3(shift)]
        rows.append(zero_rows(37, tile))
        feature_ref[start : start + tile, :] = jnp.concatenate(rows, 0).T.astype(bf16)


def panel_features(geometry):
    centre, normal = geometry[0:3], geometry[3:6]
    width = geometry.shape[1]
    scale = turns * turns
    cross = jnp.concatenate(
        [centre[0:1] * (-2.0 * scale), centre[1:3] * (-2.0 * beta_sq * scale)], 0
    )
    square = scale * (
        centre[0:1] * centre[0:1]
        + beta_sq * (centre[1:2] * centre[1:2] + centre[2:3] * centre[2:3])
    )
    product = centre * normal
    offset = (-turns) * (product[0:1] + product[1:2] + product[2:3])
    shift = (mach_number * turns) * centre[0:1]
    ch, cm, cl = split3(cross)
    nh, nm, nl = split3(turns * normal)
    ones = jnp.ones((3, width), f32)

    def stack(*rows):
        used = sum(row.shape[0] for row in rows)
        return jnp.concatenate([*rows, zero_rows(64 - used, width)], 0).astype(bf16)

    distance = stack(ch, cm, ch, cl, cm, ch, *split3(square), ones)
    along = stack(nh, nm, nh, nl, nm, nh, *split3(offset))
    moved = stack(zero_rows(18, width), *split3(shift), zero_rows(3, width), ones)
    return distance, along, moved


def kernel_values(distance, along, moved):
    inverse = lax.rsqrt(distance)
    phase = distance * inverse + moved
    part = phase - jnp.round(phase)
    square = part * part
    a0, a1, a2, a3 = scaled_sine
    sine = part * (a0 + square * (a1 + square * (a2 + square * a3)))
    cos_all = strength - sine * sine
    rest = cos_all + strength
    sin_all = sine * (rest * lax.rsqrt(rest))
    green_re = inverse * cos_all
    green_im = inverse * sin_all
    near = inverse * (turns / wave_number)
    normal_part = along * inverse
    part_re = normal_part * green_re
    part_im = normal_part * green_im
    dip_re = near * part_re + part_im
    dip_im = part_re - near * part_im
    return green_re, green_im, dip_re, dip_im


def fill_kernel(feature_ref, geometry, kernel_ref):
    distance_rows, along_rows, moved_rows = panel_features(geometry)
    for start in range(0, feature_ref.shape[0], chunk):
        rows = slice(start, start + chunk)
        features = feature_ref[rows]
        distance = jnp.dot(features, distance_rows, preferred_element_type=f32)
        moved = jnp.dot(features, moved_rows, preferred_element_type=f32)
        along = jnp.dot(features, along_rows, preferred_element_type=f32)
        for place, value in enumerate(kernel_values(distance, along, moved)):
            kernel_ref[rows, place * tile : (place + 1) * tile] = value.astype(bf16)


def first_kernel(core_ref, order_ref, mic_ref, geom_ref, feature_ref, kernel_ref):
    mic_features(order_ref, mic_ref, feature_ref)
    here = pl.multiple_of(core_ref[0] * (geom_ref.shape[1] // 2), tile)
    fill_kernel(feature_ref, geom_ref[:, pl.ds(here, tile)], kernel_ref)


def spectra_kernel(core_ref, own_ref, other_ref, geom_ref, feature_ref, first_ref, out_ref,
                   total_ref, *buffers):
    panels = own_ref.shape[3] // 2
    mics = feature_ref.shape[0]
    core = core_ref[0]

    def fill_weights(here, weight_ref):
        def both(part, kind):
            own = own_ref[part, kind, :, pl.ds(here, tile)]
            other = other_ref[part, kind, :, pl.ds(here, tile)]
            return [jnp.where(core == 0, own, other), jnp.where(core == 0, other, own)]

        mono_re, mono_im, dip_re, dip_im = both(0, 0), both(1, 0), both(0, 1), both(1, 1)
        blocks = (
            mono_re + mono_im,
            mono_im + [-x for x in mono_re],
            dip_re + dip_im,
            [-x for x in dip_im] + dip_re,
        )
        for place, block in enumerate(blocks):
            weight_ref[:, place * tile : (place + 1) * tile] = jnp.concatenate(block, 0)

    def product(kernel_ref, weight_ref):
        return lax.dot_general(
            kernel_ref[...], weight_ref[...], (((1,), (1,)), ((), ())), preferred_element_type=f32
        )

    fill_weights(pl.multiple_of(core * panels, tile), buffers[1])
    total_ref[...] = product(first_ref, buffers[1])

    def step(index, carry):
        for part in range(unroll):
            kernel_ref, weight_ref = buffers[2 * (part % 2) : 2 * (part % 2) + 2]
            block = unroll * index + part + 1
            here = pl.multiple_of(core * panels + block * tile, tile)
            fill_weights(here, weight_ref)
            fill_kernel(feature_ref, geom_ref[:, pl.ds(here, tile)], kernel_ref)
            total_ref[...] += product(kernel_ref, weight_ref)
        return carry

    lax.fori_loop(0, (panels // tile - 1) // unroll, step, 0)
    half = mics // 2
    both_halves = jnp.concatenate([total_ref[:half], total_ref[half:]], 1)
    out_ref[...] = both_halves.reshape(out_ref.shape)


vmem = pl.BlockSpec(memory_space=pltpu.VMEM)
smem = pl.BlockSpec(memory_space=pltpu.SMEM)


def prepared(core, geometry, mic_pos, order):
    mics = mic_pos.shape[1]
    return pl.pallas_call(
        first_kernel,
        out_shape=[
            jax.ShapeDtypeStruct((mics, 64), bf16),
            jax.ShapeDtypeStruct((mics, 4 * tile), bf16),
        ],
        in_specs=[smem] + [vmem] * 3,
        out_specs=[vmem] * 2,
        compiler_params=pltpu.CompilerParams(vmem_limit_bytes=16 << 20),
        cost_estimate=pl.CostEstimate(
            flops=2 * 10**9, bytes_accessed=3000000, transcendentals=0
        ),
    )(core, order, mic_pos, geometry)


def partial_spectra(core, own, other, geometry, features, first):
    mics = features.shape[0]
    return pl.pallas_call(
        spectra_kernel,
        out_shape=jax.ShapeDtypeStruct((32, mics // 64, 128), f32),
        in_specs=[smem] + [vmem] * 5,
        out_specs=vmem,
        scratch_shapes=[pltpu.VMEM((mics, 64), f32)]
        + [pltpu.VMEM((mics, 4 * tile), bf16), pltpu.VMEM((64, 4 * tile), bf16)] * 2,
        compiler_params=pltpu.CompilerParams(vmem_limit_bytes=32 << 20),
    )(core, own, other, geometry, features, first)


def shards(sources, panel_geom, mic_pos, mic_order):
    core = lax.axis_index("core")
    other = lax.ppermute(sources, "core", [(0, 1), (1, 0)])
    order = mic_order.reshape(2, 2, 32, 8).transpose(0, 2, 1, 3).reshape(1, -1)
    which = core.astype(jnp.int32).reshape(1)
    features, first = prepared(which, panel_geom, mic_pos, order)
    partial = partial_spectra(which, sources, other, panel_geom, features, first)
    kept = jnp.sum(lax.all_to_all(partial, ("z", "x"), 0, 0, tiled=True), axis=0)
    quarters = kept.reshape(2, 8, 2, 64).transpose(2, 0, 1, 3).reshape(4, 8, 64)
    for_columns = jnp.repeat(quarters, 4, axis=0)
    for_rows = jnp.tile(quarters, (4, 1, 1))
    terms = jnp.concatenate([for_columns, for_rows], 2)
    terms = lax.all_to_all(terms, ("yh", "core", "yl"), 0, 0, tiled=True)
    joined = jnp.sum(terms.reshape(2, 8, 8, 128), axis=1)
    rows = joined[:, :, 64:]
    own_columns = joined[:, :, :64].transpose(1, 0, 2).reshape(8, 128)
    spread = jnp.broadcast_to(own_columns[None], (32, 8, 128))
    columns = lax.all_to_all(spread, ("z", "x"), 0, 0, tiled=True).reshape(256, 128)
    rows, columns = lax.optimization_barrier((rows, columns))
    turned = jnp.concatenate([rows[..., 32:], -rows[..., :32]], 2)
    left = jnp.concatenate([rows, turned], 1).transpose(1, 0, 2).reshape(16, 128)
    csm = lax.dot_general(
        left, columns, (((1,), (1,)), ((), ())), precision=lax.Precision.HIGHEST
    )
    return csm.reshape(2, 8, -1) / 64


def solution(mesh):
    fine = Mesh(mesh.devices.reshape(2, 2, 4, 8, 4), ("yh", "core", *PAN))
    seg = ("yh", "core")
    placed = (P(None, None, seg, PAN), P(None, PAN), P(), P())
    return jax.shard_map(
        shards, mesh=fine, in_specs=placed, out_specs=P(None, PAN, seg), check_vma=False
    )
```

```python
import functools
import math

import jax
import jax.numpy as jnp
from jax import lax
from jax.experimental import pallas as pl
from jax.experimental.pallas import tpu as pltpu
from jax.sharding import Mesh, PartitionSpec as P

mach_number = 0.3
beta_sq = 0.91
wave_number = 40.0
turns = wave_number / (beta_sq * 2.0 * math.pi)
half_sine = (4.44284725189209, -7.306909084320068, 3.5908987522125244, -0.7760252356529236)
strength = turns / (4.0 * math.pi)
scaled_sine = tuple(math.sqrt(strength) * value for value in half_sine)

f32 = jnp.float32
bf16 = jnp.bfloat16
PAN = ("yl", "z", "x")
tile = 256
chunk = 512
unroll = 4


def split3(value):
    high = value.astype(bf16).astype(f32)
    rest = value - high
    middle = rest.astype(bf16).astype(f32)
    return high, middle, (rest - middle).astype(bf16).astype(f32)


def zero_rows(count, width):
    return jnp.zeros((count, width), f32)


def mic_features(order_ref, mic_ref, feature_ref, placed_ref):
    mics = mic_ref[...]
    total = mics.shape[1]
    parts = jnp.concatenate([*split3(mics), zero_rows(7, total)], 0).astype(bf16)
    for start in range(0, total, tile):
        wanted = order_ref[:, start : start + tile]
        ids = lax.broadcasted_iota(jnp.int32, (total, tile), 0)
        chosen = jnp.where(ids == wanted, 1.0, 0.0).astype(bf16)
        picked = jnp.dot(parts, chosen, preferred_element_type=f32)
        high, middle, low = picked[0:3], picked[3:6], picked[6:9]
        full = high + middle + low
        square = (turns * turns) * (
            full[0:1] * full[0:1] + beta_sq * (full[1:2] * full[1:2] + full[2:3] * full[2:3])
        )
        shift = (-mach_number * turns) * full[0:1]
        ones = jnp.ones((3, tile), f32)
        rows = [high, high, middle, high, middle, low, ones, *split3(square), *split3(shift)]
        rows.append(zero_rows(37, tile))
        yl = start // tile
        placed_ref[yl // 2, :, yl % 2] = jnp.concatenate(rows, 0).T.reshape(-1, 8, 64)
    feature_ref[...] = placed_ref[...].reshape(total, 64).astype(bf16)


def panel_features(geometry):
    centre, normal = geometry[0:3], geometry[3:6]
    width = geometry.shape[1]
    scale = turns * turns
    cross = jnp.concatenate(
        [centre[0:1] * (-2.0 * scale), centre[1:3] * (-2.0 * beta_sq * scale)], 0
    )
    square = scale * (
        centre[0:1] * centre[0:1]
        + beta_sq * (centre[1:2] * centre[1:2] + centre[2:3] * centre[2:3])
    )
    product = centre * normal
    offset = (-turns) * (product[0:1] + product[1:2] + product[2:3])
    shift = (mach_number * turns) * centre[0:1]
    ch, cm, cl = split3(cross)
    nh, nm, nl = split3(turns * normal)
    ones = jnp.ones((3, width), f32)

    def stack(*rows):
        used = sum(row.shape[0] for row in rows)
        return jnp.concatenate([*rows, zero_rows(64 - used, width)], 0).astype(bf16)

    distance = stack(ch, cm, ch, cl, cm, ch, *split3(square), ones)
    along = stack(nh, nm, nh, nl, nm, nh, *split3(offset))
    moved = stack(zero_rows(18, width), *split3(shift), zero_rows(3, width), ones)
    return distance, along, moved


def kernel_values(distance, along, moved):
    inverse = lax.rsqrt(distance)
    phase = distance * inverse + moved
    part = phase - jnp.round(phase)
    square = part * part
    a0, a1, a2, a3 = scaled_sine
    sine = part * (a0 + square * (a1 + square * (a2 + square * a3)))
    cos_all = strength - sine * sine
    rest = cos_all + strength
    sin_all = sine * (rest * lax.rsqrt(rest))
    green_re = inverse * cos_all
    green_im = inverse * sin_all
    near = inverse * (turns / wave_number)
    normal_part = along * inverse
    part_re = normal_part * green_re
    part_im = normal_part * green_im
    dip_re = near * part_re + part_im
    dip_im = part_re - near * part_im
    return green_re, green_im, dip_re, dip_im


def spectra_kernel(core_ref, own_ref, other_ref, geom_ref, feature_ref, out_ref, total_ref,
                   *buffers):
    panels = own_ref.shape[3] // 2
    mics = feature_ref.shape[0]
    core = core_ref[0]
    total_ref[...] = jnp.zeros_like(total_ref)

    def block_of_panels(index, kernel_ref, weight_ref):
        here = pl.multiple_of(core * panels + index * tile, tile)
        distance_rows, along_rows, moved_rows = panel_features(geom_ref[:, pl.ds(here, tile)])

        def both(part, kind):
            own = own_ref[part, kind, :, pl.ds(here, tile)]
            other = other_ref[part, kind, :, pl.ds(here, tile)]
            return [jnp.where(core == 0, own, other), jnp.where(core == 0, other, own)]

        mono_re, mono_im, dip_re, dip_im = both(0, 0), both(1, 0), both(0, 1), both(1, 1)
        blocks = (
            mono_re + mono_im,
            mono_im + [-x for x in mono_re],
            dip_re + dip_im,
            [-x for x in dip_im] + dip_re,
        )
        for place, block in enumerate(blocks):
            weight_ref[:, place * tile : (place + 1) * tile] = jnp.concatenate(block, 0)
        for start in range(0, mics, chunk):
            rows = slice(start, start + chunk)
            features = feature_ref[rows]
            distance = jnp.dot(features, distance_rows, preferred_element_type=f32)
            moved = jnp.dot(features, moved_rows, preferred_element_type=f32)
            along = jnp.dot(features, along_rows, preferred_element_type=f32)
            for place, value in enumerate(kernel_values(distance, along, moved)):
                kernel_ref[rows, place * tile : (place + 1) * tile] = value.astype(bf16)
        total_ref[...] += lax.dot_general(
            kernel_ref[...], weight_ref[...], (((1,), (1,)), ((), ())), preferred_element_type=f32
        )

    def step(index, carry):
        for part in range(unroll):
            kernel_ref, weight_ref = buffers[2 * (part % 2) : 2 * (part % 2) + 2]
            block_of_panels(unroll * index + part, kernel_ref, weight_ref)
        return carry

    lax.fori_loop(0, panels // (unroll * tile), step, 0)
    half = mics // 2
    both_halves = jnp.concatenate([total_ref[:half], total_ref[half:]], 1)
    out_ref[...] = both_halves.reshape(out_ref.shape)


vmem = pl.BlockSpec(memory_space=pltpu.VMEM)
smem = pl.BlockSpec(memory_space=pltpu.SMEM)


def prepared(mic_pos, order):
    mics = mic_pos.shape[1]
    return pl.pallas_call(
        mic_features,
        out_shape=jax.ShapeDtypeStruct((mics, 64), bf16),
        in_specs=[vmem] * 2,
        out_specs=vmem,
        scratch_shapes=[pltpu.VMEM((2, mics // 32, 2, 8, 64), f32)],
        compiler_params=pltpu.CompilerParams(vmem_limit_bytes=16 << 20),
        cost_estimate=pl.CostEstimate(
            flops=2 * 10**9, bytes_accessed=300000, transcendentals=0
        ),
    )(order, mic_pos)


def partial_spectra(core, own, other, geometry, features):
    mics = features.shape[0]
    return pl.pallas_call(
        spectra_kernel,
        out_shape=jax.ShapeDtypeStruct((32, mics // 64, 128), f32),
        in_specs=[smem] + [vmem] * 4,
        out_specs=vmem,
        scratch_shapes=[pltpu.VMEM((mics, 64), f32)]
        + [pltpu.VMEM((mics, 4 * tile), bf16), pltpu.VMEM((64, 4 * tile), bf16)] * 2,
        compiler_params=pltpu.CompilerParams(vmem_limit_bytes=32 << 20),
    )(core, own, other, geometry, features)


def shards(sources, panel_geom, mic_pos, mic_order):
    core = lax.axis_index("core")
    other = lax.ppermute(sources, "core", [(0, 1), (1, 0)])
    order = mic_order.reshape(1, -1)
    which = core.astype(jnp.int32).reshape(1)
    features = prepared(mic_pos, order)
    partial = partial_spectra(which, sources, other, panel_geom, features)
    kept = jnp.sum(lax.all_to_all(partial, ("z", "x"), 0, 0, tiled=True), axis=0)
    quarters = kept.reshape(2, 8, 2, 64).transpose(2, 0, 1, 3).reshape(4, 8, 64)
    for_columns = jnp.repeat(quarters, 4, axis=0)
    for_rows = jnp.tile(quarters, (4, 1, 1))
    terms = jnp.concatenate([for_columns, for_rows], 2)
    terms = lax.all_to_all(terms, ("yh", "core", "yl"), 0, 0, tiled=True)
    joined = jnp.sum(terms.reshape(2, 8, 8, 128), axis=1)
    rows = joined[:, :, 64:]
    own_columns = joined[:, :, :64].transpose(1, 0, 2).reshape(8, 128)
    spread = jnp.broadcast_to(own_columns[None], (32, 8, 128))
    columns = lax.all_to_all(spread, ("z", "x"), 0, 0, tiled=True).reshape(256, 128)
    rows, columns = lax.optimization_barrier((rows, columns))
    turned = jnp.concatenate([rows[..., 32:], -rows[..., :32]], 2)
    left = jnp.concatenate([rows, turned], 1).transpose(1, 0, 2).reshape(16, 128)
    csm = lax.dot_general(
        left, columns, (((1,), (1,)), ((), ())), precision=lax.Precision.HIGHEST
    )
    return csm.reshape(2, 8, -1) / 64


def solution(mesh):
    fine = Mesh(mesh.devices.reshape(2, 2, 4, 8, 4), ("yh", "core", *PAN))
    seg = ("yh", "core")
    placed = (P(None, None, seg, PAN), P(None, PAN), P(), P())
    return jax.shard_map(
        shards, mesh=fine, in_specs=placed, out_specs=P(None, PAN, seg), check_vma=False
    )
```
